256 devices in a mesh: rep: 4 (over y_hi, core), ep: 64 (over y_lo, z, x).
Axes of the slice: x: 4, y: 4 (y_hi: 2, y_lo: 2; y = y_hi * 2 + y_lo), z: 8, core: 2. Of those that a mesh axis runs over, the one named last changes fastest.
Arguments:
- tokens: bfloat16 [196608, 2048], P(('rep', 'ep')), may hold values from -6 to 6
- route: int32 [2, 131072], P(None, ('rep', 'ep')), may hold values from 0 to 767, as said below
- cotangent: bfloat16 [2, 131072, 512], P(None, ('rep', 'ep')), may hold values from -6 to 6
- weight: float32 [2, 2048, 512], P(None, 'ep'), may hold values from -0.125 to 0.125
- first_q: int32 [2, 2048, 512], P(None, 'ep'), may hold values from -127 to 127
- first_scale: float32 [2, 2048, 4], P(None, 'ep'), may hold values from 3e-05 to 6e-05
- second_q: int32 [2, 2048, 512], P(None, 'ep'), may hold values from 32 to 127
- second_scale: float32 [2, 2048, 4], P(None, 'ep'), may hold values from 3e-09 to 8e-09
Outputs:
- token_grad: bfloat16 [196608, 2048], P(('rep', 'ep'))
- step_dir: float32 [2, 2048, 512], P(None, 'ep')
- new_weight: float32 [2, 2048, 512], P(None, 'ep')
- next_gate: bfloat16 [2, 131072, 512], P(None, ('rep', 'ep'))
The draws below stay inside these ranges and needn't reach their ends.
Inputs may be any that keep to these rules, and one draw needn't show every extreme that they name: `route`: for each hot expert, the 512 entries of one device's rows (aligned blocks of 512 along the last dimension) are distinct.
All inputs are finite; a program needn't handle non-finite values.
Results may differ from the reference program's by a relative error of at most 0.006.
Values may be sent and summed in bfloat16 or wider, within the bound.
No kernel may reach another device: no remote copies, remote signals or barrier semaphores. Data moves between devices by JAX's collectives and lax.ppermute only.
A program may use at most 128 MiB of HBM per device.

```python
import math
import jax
import jax.numpy as jnp
from jax import lax

D = 2048
F = 512
HOT = 2
QBLOCK = 128
ROWS = 512
TOK_DEV = 768
TOKENS = 196608
ALL_ROWS = 131072
N_REP = 4
N_EP = 64


def draw_route(key, part):
    subkeys = jax.random.split(key, HOT * N_REP * N_EP)
    chosen_rows = jax.vmap(lambda one_key: jax.random.permutation(one_key, TOK_DEV)[:ROWS])(subkeys)
    shaped = chosen_rows.reshape(N_REP * N_EP, HOT, ROWS).transpose(1, 0, 2)
    return shaped.reshape(HOT, N_REP * N_EP * ROWS).astype(jnp.int32)


def set_ends(result, key, least, high):
    longest = result.shape.index(max(result.shape))
    spots = []
    for shift in (0, 1):
        where = [jax.random.randint(jax.random.fold_in(key, axis), (), 0, length) for axis, length in enumerate(result.shape)]
        where[longest] = (where[longest] + shift) % result.shape[longest]
        spots.append(tuple(where))
    return result.at[spots[0]].set(least).at[spots[1]].set(high)


def block_levels(rng, extent, cuts, low, largest):
    def one(axis_at, shards_of):
        draws = jax.random.uniform(jax.random.fold_in(jax.random.fold_in(rng, 6), axis_at), (shards_of,), jnp.float32, low / len(cuts), largest / len(cuts))
        return jnp.repeat(jnp.exp(draws), extent[axis_at] // shards_of).reshape((-1,) + (1,) * (len(extent) - axis_at - 1))

    gain = one(*cuts[0])
    for cut in cuts[1:]:
        gain = gain * one(*cut)
    return gain


def noise(key, shape, deviation, bound, cuts=(), held_as=jnp.bfloat16):
    loudness = block_levels(key, shape, cuts, -0.22, 0.18) if cuts else 1.0
    drawn = jax.random.normal(key, shape, jnp.float32) * deviation * loudness
    return jnp.minimum(jnp.maximum(drawn, -bound), bound).astype(held_as)


def setup_inputs(seed: int = 0) -> dict:
    streams_of = jax.random.split(jax.random.key(seed), 9)
    return {
        "tokens": noise(streams_of[0], (TOKENS, D), 1.0, 6.0, ((0, 256),)),
        "route": draw_route(jax.random.fold_in(streams_of[8], 71), 0),
        "cotangent": noise(streams_of[2], (HOT, ALL_ROWS, F), 1.0, 6.0, ((1, 256),)),
        "weight": noise(streams_of[3], (HOT, D, F), D ** -0.5, 0.125, ((1, 64),), jnp.float32),
        "first_q": set_ends(jax.random.randint(streams_of[4], (HOT, D, F), -127, 128), jax.random.fold_in(streams_of[4], 1), -127, 127).astype(jnp.int32),
        "first_scale": jnp.clip(jnp.exp(math.log(5.999999848427251e-05) - 0.6931472 * jax.random.uniform(streams_of[5], (HOT, D, F // QBLOCK), jnp.float32) ** block_levels(streams_of[5], (HOT, D, F // QBLOCK), ((1, 64),), -0.2, 0.2)), 2.9999999242136255e-05, 5.999999848427251e-05),
        "second_q": set_ends(jax.random.randint(streams_of[6], (HOT, D, F), 32, 128), jax.random.fold_in(streams_of[6], 1), 32, 127).astype(jnp.int32),
        "second_scale": jnp.clip(jnp.exp(math.log(7.999999773744548e-09) - 0.98082922 * jax.random.uniform(streams_of[7], (HOT, D, F // QBLOCK), jnp.float32) ** block_levels(streams_of[7], (HOT, D, F // QBLOCK), ((1, 64),), -0.2, 0.2)), 3.000000026176508e-09, 7.999999773744548e-09),
    }


BETA_ONE = 0.9
BETA_TWO = 0.95
CORR_ONE = 1.0 - 0.9 ** 10
CORR_TWO = 1.0 - 0.95 ** 10
EPSILON = 1e-08
RATE = 0.002

def dequant(quant, scale):
    shaped = quant.astype(jnp.float32).reshape(quant.shape[0], quant.shape[1], -1, QBLOCK)
    return (shaped * scale[..., None]).reshape(quant.shape)

def adam_update(weight, grad, first_q, first_scale, second_q, second_scale):
    first = BETA_ONE * dequant(first_q, first_scale) + (1.0 - BETA_ONE) * grad
    second = BETA_TWO * dequant(second_q, second_scale) + (1.0 - BETA_TWO) * grad * grad
    step = first / CORR_ONE / (jnp.sqrt(second / CORR_TWO) + EPSILON)
    return (step, weight - RATE * step)

def reference(tokens, route, cotangent, weight, first_q, first_scale, second_q, second_scale):
    devices = N_REP * N_EP
    pool = tokens.reshape(devices, TOK_DEV, D)
    routes = route.reshape(HOT, devices, ROWS).transpose(1, 0, 2)
    cots = cotangent.reshape(HOT, devices, ROWS, F).transpose(1, 0, 2, 3)
    weight_b = weight.astype(jnp.bfloat16).astype(jnp.float32)
    high = lax.Precision.HIGHEST

    def one_device(total, items):
        pool_dev, route_dev, cot_dev = items
        chosen = pool_dev[route_dev].astype(jnp.float32)
        gate = jnp.einsum('erd,edf->erf', chosen, weight_b, precision=high)
        sig = jax.nn.sigmoid(gate)
        dgate = (cot_dev.astype(jnp.float32) * sig * (1.0 + gate * (1.0 - sig))).astype(jnp.bfloat16).astype(jnp.float32)
        dx = jnp.einsum('erf,edf->erd', dgate, weight_b, precision=high)
        grads = jnp.zeros((TOK_DEV, D), jnp.float32).at[route_dev.reshape(-1)].add(dx.reshape(-1, D))
        total = total + jnp.einsum('erd,erf->edf', chosen, dgate, precision=high)
        return (total, grads.astype(jnp.bfloat16))
    summed, token_grad = lax.scan(one_device, jnp.zeros((HOT, D, F), jnp.float32), (pool, routes, cots))
    grad = summed / ALL_ROWS
    step_dir, new_weight = adam_update(weight, grad, first_q, first_scale, second_q, second_scale)
    new_b = new_weight.astype(jnp.bfloat16).astype(jnp.float32)

    def rerun(items):
        pool_dev, route_dev = items
        chosen = pool_dev[route_dev].astype(jnp.float32)
        return jnp.einsum('erd,edf->erf', chosen, new_b, precision=high).astype(jnp.bfloat16)
    nexts = lax.map(rerun, (pool, routes))
    next_gate = nexts.transpose(1, 0, 2, 3).reshape(HOT, ALL_ROWS, F)
    return (token_grad.reshape(TOKENS, D), step_dir, new_weight, next_gate)
```

```python
import jax
import jax.numpy as jnp
from jax import lax
from jax.sharding import Mesh
from jax.sharding import PartitionSpec as P

QBLOCK = 128

BETA_ONE = 0.9
BETA_TWO = 0.95
CORR_ONE = 1.0 - 0.9**10
CORR_TWO = 1.0 - 0.95**10
EPSILON = 1e-08
RATE = 0.002

BF = jnp.bfloat16
F32 = jnp.float32
XY = ("yh", "yl", "x")


def dequant(quant, scale):
    shaped = quant.astype(F32).reshape(quant.shape[0], quant.shape[1], -1, QBLOCK)
    return (shaped * scale[..., None]).reshape(quant.shape)


def adam_update(weight, grad, first_q, first_scale, second_q, second_scale):
    first = BETA_ONE * dequant(first_q, first_scale) + (1.0 - BETA_ONE) * grad
    second = BETA_TWO * dequant(second_q, second_scale) + (1.0 - BETA_TWO) * grad * grad
    step = first / CORR_ONE / (jnp.sqrt(second / CORR_TWO) + EPSILON)
    return (step, weight - RATE * step)


def swap(value):
    return lax.ppermute(value, "core", [(0, 1), (1, 0)])


def spread(block, axes, count):
    return lax.all_to_all(
        jnp.broadcast_to(block[None], (count,) + block.shape), axes, 0, 0, tiled=True
    )


def gather_rows(block, n_z, n_xy):
    rows, feature = block.shape
    along_z = spread(block, "z", n_z)
    whole = spread(along_z, XY, n_xy)
    n_x = lax.axis_size("x")
    whole = whole.reshape(2, 2, n_x, n_z, rows, feature).transpose(1, 3, 2, 0, 4, 5)
    return whole.reshape(-1, feature)


def reduce_rows(grad, n_z, n_xy):
    depth, feature = grad.shape
    n_x = lax.axis_size("x")
    rows = depth // (n_z * n_xy)
    blocks = grad.reshape(2, n_z, n_x, 2, rows, feature).transpose(3, 0, 2, 1, 4, 5)
    blocks = blocks.reshape(n_xy, n_z, rows, feature)
    got = lax.all_to_all(blocks.astype(BF), XY, 0, 0, tiled=True)
    part = jnp.sum(got.astype(F32), axis=0).astype(BF)
    got = lax.all_to_all(part, "z", 0, 0, tiled=True)
    return jnp.sum(got.astype(F32), axis=0)


def pair(mine, other, core):
    return jnp.where(core == 0, jnp.stack([mine, other]), jnp.stack([other, mine]))


def on_device(tokens, route, cotangent, weight, first_q, first_scale, second_q, second_scale):
    n_rep = lax.axis_size("yh") * lax.axis_size("core")
    n_z = lax.axis_size("z")
    n_xy = lax.axis_size(XY)
    core = lax.axis_index("core")
    high = lax.axis_index("yh")
    rows_here = route.shape[1]
    total_rows = rows_here * n_rep * lax.axis_size("yl") * n_z * lax.axis_size("x")
    owned = weight.shape[1]
    half = owned // 2

    def mine_of(array):
        return lax.dynamic_index_in_dim(array, core, 0, keepdims=False)

    def other_of(array):
        return lax.dynamic_index_in_dim(array, 1 - core, 0, keepdims=False)

    def part_of(array):
        picked = mine_of(array)
        return lax.dynamic_slice_in_dim(picked, high * half, half, 0)

    weight_part = part_of(weight)
    whole = gather_rows(weight_part.astype(BF), n_z, n_xy)
    route_mine = mine_of(route)
    route_other = other_of(route)
    chosen = jnp.concatenate([tokens[route_mine], swap(tokens[route_other])], axis=0)
    cot = jnp.concatenate([mine_of(cotangent), swap(other_of(cotangent))], axis=0)

    gate = jnp.dot(chosen, whole, preferred_element_type=F32)
    sig = jax.nn.sigmoid(gate)
    dgate = (cot.astype(F32) * sig * (1.0 + gate * (1.0 - sig))).astype(BF)
    grad_all = jnp.einsum("rd,rf->df", chosen, dgate, preferred_element_type=F32)
    grad = reduce_rows(grad_all, n_z, n_xy) / total_rows

    def quarter(array):
        return part_of(array)[None]

    _, new_part = adam_update(
        weight_part[None], grad[None], quarter(first_q), quarter(first_scale), quarter(second_q), quarter(second_scale)
    )
    new_whole = gather_rows(new_part[0].astype(BF), n_z, n_xy)
    nexts = jnp.dot(chosen, new_whole, preferred_element_type=F32).astype(BF)
    next_gate = pair(nexts[:rows_here], swap(nexts[rows_here:]), core)

    both = pair(grad, swap(grad), core)
    far = lax.ppermute(both, "yh", [(0, 1), (1, 0)])
    both = jnp.where(
        high == 0, jnp.concatenate([both, far], axis=1), jnp.concatenate([far, both], axis=1)
    )
    step_dir, new_weight = adam_update(weight, both, first_q, first_scale, second_q, second_scale)

    places = jnp.arange(tokens.shape[0], dtype=jnp.int32)

    def at_tokens(routes, rows):
        hot = (places[:, None] == routes[None, :]).astype(BF)
        return jnp.dot(hot, rows, preferred_element_type=F32).astype(BF)

    other_whole = swap(whole)
    other_rows = swap(dgate[rows_here:])
    token_grad = (
        jnp.einsum("tf,df->td", at_tokens(route_mine, dgate[:rows_here]), whole, preferred_element_type=F32)
        + jnp.einsum("tf,df->td", at_tokens(route_other, other_rows), other_whole, preferred_element_type=F32)
    ).astype(BF)
    return (token_grad, step_dir, new_weight, next_gate)


def solution(mesh):
    split = Mesh(mesh.devices.reshape(2, 2, 2, 8, 4), ("yh", "core", "yl", "z", "x"))
    rep = ("yh", "core")
    ep = ("yl", "z", "x")
    every = rep + ep
    in_specs = (
        P(every, None),
        P(None, every),
        P(None, every, None),
        P(None, ep, None),
        P(None, ep, None),
        P(None, ep, None),
        P(None, ep, None),
        P(None, ep, None),
    )
    out_specs = (
        P(every, None),
        P(None, ep, None),
        P(None, ep, None),
        P(None, every, None),
    )
    return jax.shard_map(
        on_device, mesh=split, in_specs=in_specs, out_specs=out_specs, check_vma=False
    )
```

```python
import functools

import jax
import jax.numpy as jnp
from jax import lax
from jax.experimental import pallas as pl
from jax.experimental.pallas import tpu as pltpu
from jax.sharding import Mesh
from jax.sharding import PartitionSpec as P

QBLOCK = 128

BETA_ONE = 0.9
BETA_TWO = 0.95
CORR_ONE = 1.0 - 0.9**10
CORR_TWO = 1.0 - 0.95**10
EPSILON = 1e-08
RATE = 0.002

BF = jnp.bfloat16
F32 = jnp.float32
XY = ("yh", "yl", "x")


def dequant(quant, scale):
    shaped = quant.astype(F32).reshape(quant.shape[0], quant.shape[1], -1, QBLOCK)
    return (shaped * scale[..., None]).reshape(quant.shape)


def adam_update(weight, grad, first_q, first_scale, second_q, second_scale):
    first = BETA_ONE * dequant(first_q, first_scale) + (1.0 - BETA_ONE) * grad
    second = BETA_TWO * dequant(second_q, second_scale) + (1.0 - BETA_TWO) * grad * grad
    step = first / CORR_ONE / (jnp.sqrt(second / CORR_TWO) + EPSILON)
    return (step, weight - RATE * step)


def swap(value):
    return lax.ppermute(value, "core", [(0, 1), (1, 0)])


def in_hbm(value):
    return pltpu.with_memory_space_constraint(value, pltpu.HBM)


def call(kernel, outs, *args, scratch=(), mib=8, places=None):
    vmem = pl.BlockSpec(memory_space=pltpu.VMEM)
    any_place = pl.BlockSpec(memory_space=pl.ANY)
    return pl.pallas_call(
        kernel,
        out_shape=[
            jax.ShapeDtypeStruct(shape, dtype) if near else pltpu.HBM(shape, dtype)
            for shape, dtype, near in outs
        ],
        in_specs=[
            pl.BlockSpec(memory_space=pltpu.SMEM) if near is None else vmem if near else any_place
            for near in (places or [True] * len(args))
        ],
        out_specs=[vmem if near else any_place for _, _, near in outs],
        scratch_shapes=list(scratch),
        compiler_params=pltpu.CompilerParams(vmem_limit_bytes=mib << 20),
    )(*args)


def repeat_kernel(in_ref, out_ref, sems):
    copies = [pltpu.make_async_copy(in_ref, out_ref.at[k], sems.at[k]) for k in range(out_ref.shape[0])]
    for copy in copies:
        copy.start()
    for copy in copies:
        copy.wait()


def repeat(block, count):
    return call(
        repeat_kernel,
        [((count,) + block.shape, BF, False)],
        block,
        scratch=[pltpu.SemaphoreType.DMA((count,))],
    )[0]


def natural_order(gathered_ref, whole_ref, n_z):
    n_xy, many, _ = gathered_ref.shape
    rows = many // n_z
    n_x = n_xy // 4
    for high in range(2):
        for low in range(2):
            for x in range(n_x):
                for z in range(n_z):
                    at = (((low * n_z + z) * n_x + x) * 2 + high) * rows
                    whole_ref[at : at + rows, :] = gathered_ref[
                        (high * 2 + low) * n_x + x, z * rows : (z + 1) * rows
                    ]


def across_kernel(mine_ref, other_ref, across_ref, buf_ref, sems):
    count, depth = mine_ref.shape
    step = 256
    copies = []
    for d in range(0, depth, step):
        for base, in_ref in ((0, mine_ref), (count, other_ref)):
            buf_ref[d : d + step, base : base + count] = in_ref[:, d : d + step].T
        at = pl.ds(d, step)
        copies.append(pltpu.make_async_copy(buf_ref.at[at], across_ref.at[at], sems.at[d // step]))
        copies[-1].start()
    for copy in copies:
        copy.wait()


def gate_kernel(core_ref, mine_ref, other_ref, cot_mine_ref, cot_other_ref, across_ref, gathered_ref,
                blocks_ref, dmine_ref, dother_ref, whole_out_ref,
                whole_ref, x_ref, cot_ref, turned_ref, d_ref, part_ref, in_sems, w_sems, out_sems):
    low_n, n_z, n_x, high_n, rows, feature = whole_ref.shape
    count, depth = mine_ref.shape
    step = 256
    core = core_ref[0]
    w_copies = []
    for high in range(high_n):
        for low in range(low_n):
            for x in range(n_x):
                k = (high * low_n + low) * n_x + x
                w_copies.append(
                    pltpu.make_async_copy(gathered_ref.at[k], whole_ref.at[low, :, x, high], w_sems.at[k])
                )
    loads = [
        pltpu.make_async_copy(mine_ref, x_ref.at[pl.ds(0, count)], in_sems.at[0]),
        pltpu.make_async_copy(cot_mine_ref.at[core], cot_ref.at[pl.ds(0, count)], in_sems.at[1]),
        pltpu.make_async_copy(other_ref, x_ref.at[pl.ds(count, count)], in_sems.at[2]),
        pltpu.make_async_copy(cot_other_ref.at[core], cot_ref.at[pl.ds(count, count)], in_sems.at[3]),
        pltpu.make_async_copy(across_ref, turned_ref, in_sems.at[4]),
    ]
    for copy in w_copies + loads:
        copy.start()
    for copy in w_copies:
        copy.wait()
    whole_out = pltpu.make_async_copy(whole_ref, whole_out_ref, in_sems.at[5])
    whole_out.start()
    whole = whole_ref[...].reshape(depth, feature)
    d_out = []
    for half in range(2):
        loads[2 * half].wait()
        loads[2 * half + 1].wait()
        for r in range(half * count, (half + 1) * count, step):
            gate = jnp.dot(x_ref[r : r + step, :], whole, preferred_element_type=F32)
            sig = jax.nn.sigmoid(gate)
            d_ref[r : r + step, :] = (cot_ref[r : r + step, :].astype(F32) * sig * (1.0 + gate * (1.0 - sig))).astype(BF)
        d_out.append(
            pltpu.make_async_copy(
                d_ref.at[pl.ds(half * count, count)], (dmine_ref, dother_ref)[half], in_sems.at[6 + half]
            )
        )
        d_out[-1].start()
    loads[4].wait()
    pair_rows = n_x * high_n * rows
    out_copies = []
    for low in range(low_n):
        for z in range(0, n_z, step // pair_rows):
            d = (low * n_z + z) * pair_rows
            part = jnp.dot(turned_ref[d : d + step, :], d_ref[...], preferred_element_type=F32).astype(BF)
            for k in range(step // rows):
                index = d // rows + k
                high = index % high_n
                x = index // high_n % n_x
                part_ref[(high * low_n + low) * n_x + x, index // high_n // n_x % n_z] = part[k * rows : (k + 1) * rows]
        for high in range(high_n):
            at = pl.ds((high * low_n + low) * n_x, n_x)
            out_copies.append(
                pltpu.make_async_copy(part_ref.at[at], blocks_ref.at[at], out_sems.at[high * low_n + low])
            )
            out_copies[-1].start()
    for copy in out_copies + d_out + [whole_out]:
        copy.wait()


def token_kernel(n_z, routes_ref, dmine_ref, dother_ref, whole_ref, other_ref, out_ref, other_whole_ref, placed_ref):
    natural_order(other_ref, other_whole_ref, n_z)
    count = dmine_ref.shape[0]
    step = 256
    turned = (((1,), (1,)), ((), ()))
    for t in range(0, out_ref.shape[0], step):
        places = t + lax.broadcasted_iota(jnp.int32, (step, count), 0)
        for e, d_ref in enumerate((dmine_ref, dother_ref)):
            hot = jnp.where(places == routes_ref[e : e + 1, :], 1.0, 0.0).astype(BF)
            placed_ref[e] = jnp.dot(hot, d_ref[...], preferred_element_type=F32).astype(BF)
        for d in range(0, out_ref.shape[1], 2 * step):
            at = slice(d, d + 2 * step)
            total = lax.dot_general(placed_ref[0], whole_ref[at, :], turned, preferred_element_type=F32)
            total = total + lax.dot_general(placed_ref[1], other_whole_ref[at, :], turned, preferred_element_type=F32)
            out_ref[t : t + step, at] = total.astype(BF)


def sum_kernel(got_ref, out_ref):
    total = got_ref[0].astype(F32)
    for k in range(1, got_ref.shape[0]):
        total = total + got_ref[k].astype(F32)
    out_ref[...] = total.astype(BF)


def sum_blocks(got, step=32):
    count, rows, feature = got.shape
    return pl.pallas_call(
        sum_kernel,
        grid=(rows // step,),
        in_specs=[pl.BlockSpec((count, step, feature), lambda i: (0, i, 0))],
        out_specs=pl.BlockSpec((step, feature), lambda i: (i, 0)),
        out_shape=jax.ShapeDtypeStruct((rows, feature), BF),
    )(got)


def adam_kernel(total_rows):
    def kernel(got_ref, weight_ref, first_ref, second_ref, grad_ref, out_ref):
        total = got_ref[0].astype(F32)
        for k in range(1, got_ref.shape[0]):
            total = total + got_ref[k].astype(F32)
        grad = total / total_rows
        grad_ref[...] = grad
        first = first_ref[...] + (1.0 - BETA_ONE) * grad
        second = second_ref[...] + (1.0 - BETA_TWO) * grad * grad
        step = first / CORR_ONE / (jnp.sqrt(second / CORR_TWO) + EPSILON)
        new = (weight_ref[...] - RATE * step).astype(BF)
        for k in range(out_ref.shape[0]):
            out_ref[k] = new

    return kernel


def next_other_kernel(n_z, x_ref, gathered_ref, out_ref, whole_ref):
    natural_order(gathered_ref, whole_ref, n_z)
    out_ref[...] = jnp.dot(x_ref[...], whole_ref[...], preferred_element_type=F32).astype(BF)


def next_mine_kernel(x_ref, whole_ref, out_ref):
    out_ref[...] = jnp.dot(x_ref[...], whole_ref[...], preferred_element_type=F32).astype(BF)


def pair(mine, other, core):
    return jnp.where(core == 0, jnp.stack([mine, other]), jnp.stack([other, mine]))


def on_device(tokens, route, cotangent, weight, first_q, first_scale, second_q, second_scale):
    n_rep = lax.axis_size("yh") * lax.axis_size("core")
    n_z = lax.axis_size("z")
    n_x = lax.axis_size("x")
    n_xy = lax.axis_size(XY)
    core = lax.axis_index("core")
    high = lax.axis_index("yh")
    rows_here = route.shape[1]
    depth = tokens.shape[1]
    feature = cotangent.shape[2]
    total_rows = rows_here * n_rep * lax.axis_size("yl") * n_z * n_x
    owned = weight.shape[1]
    half = owned // 2

    def mine_of(array):
        return lax.dynamic_index_in_dim(array, core, 0, keepdims=False)

    def other_of(array):
        return lax.dynamic_index_in_dim(array, 1 - core, 0, keepdims=False)

    def part_of(array):
        return lax.dynamic_slice_in_dim(mine_of(array), high * half, half, 0)

    def over_z(blocks):
        return lax.all_to_all(blocks, "z", 0, 0, tiled=True)

    def over_xy(blocks):
        flat = blocks.reshape(n_xy, n_z * half, feature)
        return lax.all_to_all(flat, XY, 0, 0, tiled=True)

    weight_part = part_of(weight)
    start_blocks = jnp.broadcast_to(weight_part.astype(BF)[None], (n_z, half, feature))
    to_send = repeat(over_z(start_blocks).reshape(-1, feature), n_xy)
    tokens_far, route_far, cot_far = swap(tokens), swap(route), swap(cotangent)
    tokens_b, route_b, tokens_far, route_far, to_send = lax.optimization_barrier(
        (tokens, route, tokens_far, route_far, to_send)
    )
    gathered = over_xy(to_send)
    route_mine = mine_of(route_b)
    route_other = other_of(route_b)
    x_other = tokens_far[mine_of(route_far)]
    x_mine = tokens_b[route_mine]
    (across,) = call(
        across_kernel,
        [((depth, 2 * rows_here), BF, False)],
        x_mine,
        x_other,
        scratch=[pltpu.VMEM((depth, 2 * rows_here), BF), pltpu.SemaphoreType.DMA((depth // 256,))],
        mib=16,
    )
    first_part = BETA_ONE * dequant(part_of(first_q)[None], part_of(first_scale)[None])[0]
    second_part = BETA_TWO * dequant(part_of(second_q)[None], part_of(second_scale)[None])[0]
    gathered, x_mine, x_other, across, cot_far, first_part, second_part = lax.optimization_barrier(
        (gathered, x_mine, x_other, across, cot_far, first_part, second_part)
    )

    other_gathered = swap(gathered)
    blocks, dmine, dother, whole = call(
        gate_kernel,
        [
            ((n_xy, n_z, half, feature), BF, False),
            ((rows_here, feature), BF, False),
            ((rows_here, feature), BF, False),
            ((2, n_z, n_x, 2, half, feature), BF, False),
        ],
        core.reshape(1),
        in_hbm(x_mine),
        in_hbm(x_other),
        in_hbm(cotangent),
        in_hbm(cot_far),
        in_hbm(across),
        in_hbm(gathered.reshape(n_xy, n_z, half, feature)),
        scratch=[
            pltpu.VMEM((2, n_z, n_x, 2, half, feature), BF),
            pltpu.VMEM((2 * rows_here, depth), BF),
            pltpu.VMEM((2 * rows_here, feature), BF),
            pltpu.VMEM((depth, 2 * rows_here), BF),
            pltpu.VMEM((2 * rows_here, feature), BF),
            pltpu.VMEM((n_xy, n_z, half, feature), BF),
            pltpu.SemaphoreType.DMA((8,)),
            pltpu.SemaphoreType.DMA((n_xy,)),
            pltpu.SemaphoreType.DMA((4,)),
        ],
        mib=24,
        places=[None] + [False] * 6,
    )
    whole = whole.reshape(depth, feature)
    got = over_xy(blocks)
    other_rows = swap(dother)
    (token_grad,) = call(
        functools.partial(token_kernel, n_z),
        [(tokens.shape, BF, True)],
        jnp.stack([route_mine, route_other]),
        dmine,
        other_rows,
        whole,
        other_gathered,
        scratch=[pltpu.VMEM((depth, feature), BF), pltpu.VMEM((2, 256, feature), BF)],
        mib=14,
    )
    got, token_grad = lax.optimization_barrier((got, token_grad))
    part = sum_blocks(got)
    got_z = over_z(part.reshape(n_z, half, feature))
    grad, new_blocks = call(
        adam_kernel(total_rows),
        [((half, feature), F32, True), ((n_z, half, feature), BF, True)],
        (got_z),
        weight_part,
        first_part,
        second_part,
    )
    new_send = repeat(over_z(new_blocks).reshape(-1, feature), n_xy)
    new_send, grad = lax.optimization_barrier((new_send, grad))
    new_gathered = over_xy(new_send)
    both = pair(grad, swap(grad), core)
    far = lax.ppermute(both, "yh", [(0, 1), (1, 0)])
    both = jnp.where(
        high == 0, jnp.concatenate([both, far], axis=1), jnp.concatenate([far, both], axis=1)
    )
    step_dir, new_weight = adam_update(weight, both, first_q, first_scale, second_q, second_scale)
    new_gathered, step_dir, new_weight = lax.optimization_barrier((new_gathered, step_dir, new_weight))

    next_other, new_whole = call(
        functools.partial(next_other_kernel, n_z),
        [((rows_here, feature), BF, True), ((depth, feature), BF, True)],
        x_other,
        (new_gathered),
    )
    next_other = swap(next_other)
    (next_mine,) = call(
        next_mine_kernel, [((rows_here, feature), BF, True)], x_mine, new_whole
    )
    next_gate = pair(next_mine, next_other, core)
    return (token_grad, step_dir, new_weight, next_gate)


def solution(mesh):
    split = Mesh(mesh.devices.reshape(2, 2, 2, 8, 4), ("yh", "core", "yl", "z", "x"))
    rep = ("yh", "core")
    ep = ("yl", "z", "x")
    every = rep + ep
    in_specs = (
        P(every, None),
        P(None, every),
        P(None, every, None),
        P(None, ep, None),
        P(None, ep, None),
        P(None, ep, None),
        P(None, ep, None),
        P(None, ep, None),
    )
    out_specs = (
        P(every, None),
        P(None, ep, None),
        P(None, ep, None),
        P(None, every, None),
    )
    return jax.shard_map(
        on_device, mesh=split, in_specs=in_specs, out_specs=out_specs, check_vma=False
    )
```

```python
import jax
import jax.numpy as jnp
from jax import lax
from jax.experimental import pallas as pl
from jax.experimental.pallas import tpu as pltpu
from jax.sharding import Mesh
from jax.sharding import PartitionSpec as P

QBLOCK = 128

BETA_ONE = 0.9
BETA_TWO = 0.95
CORR_ONE = 1.0 - 0.9**10
CORR_TWO = 1.0 - 0.95**10
EPSILON = 1e-08
RATE = 0.002

BF = jnp.bfloat16
F32 = jnp.float32
AXES = ("yh", "core", "yl", "z", "x")
N_Y = 4
N_X = 4


def dequant(quant, scale):
    shaped = quant.astype(F32).reshape(quant.shape[0], quant.shape[1], -1, QBLOCK)
    return (shaped * scale[..., None]).reshape(quant.shape)


def adam_update(weight, grad, first_q, first_scale, second_q, second_scale):
    first = BETA_ONE * dequant(first_q, first_scale) + (1.0 - BETA_ONE) * grad
    second = BETA_TWO * dequant(second_q, second_scale) + (1.0 - BETA_TWO) * grad * grad
    step = first / CORR_ONE / (jnp.sqrt(second / CORR_TWO) + EPSILON)
    return (step, weight - RATE * step)


def swap(value):
    return lax.ppermute(value, "core", [(0, 1), (1, 0)])


def cross(value, other_core):
    flip = 3 if other_core else 2
    return lax.ppermute(value, ("yh", "core"), [(i, i ^ flip) for i in range(4)])


def shift(value, k, inner):
    n_z = lax.axis_size("z")

    def number(y, core, z, x):
        return (((y // 2 * 2 + core) * 2 + y % 2) * n_z + z) * N_X + x

    pairs = []
    for core in range(2):
        for y in range(N_Y):
            for z in range(n_z):
                for x in range(N_X):
                    if (core == 0) == inner:
                        target = number(y, core, z, (x + k) % N_X)
                    else:
                        target = number((y + k) % N_Y, core, z, x)
                    pairs.append((number(y, core, z, x), target))
    return lax.ppermute(value, AXES, pairs)


def place(spot_ref, j, k, away):
    core = spot_ref[0]
    outer = (spot_ref[2] + (j if away else N_Y - j)) % N_Y
    inner = (spot_ref[1] + (k if away else N_X - k)) % N_X
    y = jnp.where(core == 0, outer, inner)
    x = jnp.where(core == 0, inner, outer)
    return y % 2, x, y // 2


def in_hbm(value):
    return pltpu.with_memory_space_constraint(value, pltpu.HBM)


ANY = "any"
SMEM = "smem"
VMEM = "vmem"


def call(kernel, outs, *args, scratch=(), mib=8, places=None):
    spec = {
        ANY: pl.BlockSpec(memory_space=pl.ANY),
        SMEM: pl.BlockSpec(memory_space=pltpu.SMEM),
        VMEM: pl.BlockSpec(memory_space=pltpu.VMEM),
    }
    return pl.pallas_call(
        kernel,
        out_shape=[
            pltpu.HBM(shape, dtype) if where == ANY else jax.ShapeDtypeStruct(shape, dtype)
            for shape, dtype, where in outs
        ],
        in_specs=[spec[where] for where in (places or [VMEM] * len(args))],
        out_specs=[spec[where] for _, _, where in outs],
        scratch_shapes=list(scratch),
        compiler_params=pltpu.CompilerParams(vmem_limit_bytes=mib << 20),
    )(*args)


def pack_kernel(*refs):
    *in_refs, out_ref = refs
    for k, in_ref in enumerate(in_refs):
        out_ref[k] = in_ref[...]


def gather_blocks(block):
    parts = [block] + [shift(block, k, True) for k in (1, 3, 2)]
    parts = [parts[0], parts[1], parts[3], parts[2]]
    (packed,) = call(pack_kernel, [((N_X,) + block.shape, BF, VMEM)], *parts)
    far = [shift(packed, k, False) for k in (1, 3, 2)]
    return [packed, far[0], far[2], far[1]]


def load_whole(spot_ref, block_refs, whole_ref, sems):
    copies = []
    for j in range(N_Y):
        for k in range(N_X):
            low, x, high = place(spot_ref, j, k, False)
            copies.append(
                pltpu.make_async_copy(
                    block_refs[j].at[k], whole_ref.at[low, :, x, high], sems.at[j * N_X + k]
                )
            )
    return copies


def rows_kernel(spot_ref, route_ref, tokens_ref, x_ref, across_ref, buf_ref, sems):
    count, depth = x_ref.shape
    low_n, n_z, n_x, high_n, rows, _ = buf_ref.shape
    step = 256
    core = spot_ref[0]
    places = lax.broadcasted_iota(jnp.int32, (tokens_ref.shape[0], count), 0)
    hot = jnp.where(places == route_ref[...], 1.0, 0.0).astype(BF).T
    copies = []
    for low in range(low_n):
        for d in range(low * depth // low_n, (low + 1) * depth // low_n, step):
            picked = jnp.dot(hot, tokens_ref[:, d : d + step], preferred_element_type=F32).astype(BF)
            x_ref[:, d : d + step] = picked
            turned = picked.T
            for g in range(step // rows):
                index = d // rows + g
                high = index % high_n
                x = index // high_n % n_x
                z = index // high_n // n_x % n_z
                buf_ref[low, z, x, high] = turned[g * rows : (g + 1) * rows]
        for high in range(high_n):
            for x in range(n_x):
                y = 2 * high + low
                j = (jnp.where(core == 0, y, x) - spot_ref[2] + N_Y) % N_Y
                k = (jnp.where(core == 0, x, y) - spot_ref[1] + N_X) % N_X
                copies.append(
                    pltpu.make_async_copy(buf_ref.at[low, :, x, high], across_ref.at[j, k], sems.at[len(copies)])
                )
                copies[-1].start()
    for copy in copies:
        copy.wait()


def gate_kernel(spot_ref, mine_ref, other_ref, cot_mine_ref, cot_other_ref,
                across_mine_ref, across_other_ref, g0, g1, g2, g3, o0, o1, o2, o3, dmine_ref, dother_ref, whole_out_ref,
                whole_ref, x_ref, cot_ref, turned_ref, d_ref, part_ref, in_sems, w_sems, t_sems, out_sems):
    low_n, n_z, n_x, high_n, rows, feature = whole_ref.shape
    count, depth = mine_ref.shape
    step = 256
    core = spot_ref[0]
    w_copies = load_whole(spot_ref, (g0, g1, g2, g3), whole_ref, w_sems)
    loads = [
        pltpu.make_async_copy(mine_ref, x_ref.at[pl.ds(0, count)], in_sems.at[0]),
        pltpu.make_async_copy(cot_mine_ref.at[core], cot_ref.at[pl.ds(0, count)], in_sems.at[1]),
        pltpu.make_async_copy(other_ref, x_ref.at[pl.ds(count, count)], in_sems.at[2]),
        pltpu.make_async_copy(cot_other_ref.at[core], cot_ref.at[pl.ds(count, count)], in_sems.at[3]),
    ]
    order = (1, 3, 2, 0)
    t_loads = [
        [
            pltpu.make_async_copy(ref.at[j], turned_ref.at[half, j], t_sems.at[half, j])
            for half, ref in enumerate((across_mine_ref, across_other_ref))
        ]
        for j in order
    ]
    for copy in w_copies + loads[:2]:
        copy.start()
    for copy in w_copies:
        copy.wait()
    for copy in loads[2:] + [copy for pair in t_loads for copy in pair]:
        copy.start()
    whole_out = pltpu.make_async_copy(whole_ref, whole_out_ref, in_sems.at[4])
    whole_out.start()
    whole = whole_ref[...].reshape(depth, feature)
    outs = [whole_out]
    for half in range(2):
        loads[2 * half].wait()
        loads[2 * half + 1].wait()
        for r in range(half * count, (half + 1) * count, step):
            gate = jnp.dot(x_ref[r : r + step, :], whole, preferred_element_type=F32)
            sig = jax.nn.sigmoid(gate)
            cot = cot_ref[r : r + step, :].astype(F32)
            d_ref[r : r + step, :] = (cot * sig * (1.0 + gate * (1.0 - sig))).astype(BF)
        outs.append(
            pltpu.make_async_copy(
                d_ref.at[pl.ds(half * count, count)], (dmine_ref, dother_ref)[half], in_sems.at[5 + half]
            )
        )
        outs[-1].start()
    for i, j in enumerate(order):
        for copy in t_loads[i]:
            copy.wait()
        for k in range(0, N_X, 2):
            part = None
            for half in range(2):
                turned = turned_ref[half, j, k : k + 2].reshape(2 * n_z * rows, count)
                product = jnp.dot(turned, d_ref[half * count : (half + 1) * count, :], preferred_element_type=F32)
                part = product if part is None else part + product
            part_ref[j, k : k + 2] = part.astype(BF).reshape(2, n_z, rows, feature)
        outs.append(pltpu.make_async_copy(part_ref.at[j], (o0, o1, o2, o3)[j], out_sems.at[j]))
        outs[-1].start()
    for copy in outs:
        copy.wait()


def token_kernel(routes_ref, dmine_ref, dother_ref, whole_ref, other_ref, out_ref, placed_ref):
    count = dmine_ref.shape[0]
    step = 256
    turned = (((1,), (1,)), ((), ()))
    for t in range(0, out_ref.shape[0], step):
        places = t + lax.broadcasted_iota(jnp.int32, (step, count), 0)
        for e, d_ref in enumerate((dmine_ref, dother_ref)):
            hot = jnp.where(places == routes_ref[e : e + 1, :], 1.0, 0.0).astype(BF)
            placed_ref[e] = jnp.dot(hot, d_ref[...], preferred_element_type=F32).astype(BF)
        for d in range(0, out_ref.shape[1], 2 * step):
            at = slice(d, d + 2 * step)
            total = lax.dot_general(placed_ref[0], whole_ref[at, :], turned, preferred_element_type=F32)
            total = total + lax.dot_general(placed_ref[1], other_ref[at, :], turned, preferred_element_type=F32)
            out_ref[t : t + step, at] = total.astype(BF)


def sum_outer_kernel(a, b, c, d, o0, o1, o2, o3):
    for k, out_ref in enumerate((o0, o1, o2, o3)):
        total = a[k].astype(F32) + b[k].astype(F32) + c[k].astype(F32) + d[k].astype(F32)
        out_ref[...] = total.astype(BF)


def sum_inner_kernel(a, b, c, d, out_ref):
    total = a[...].astype(F32) + b[...].astype(F32) + c[...].astype(F32) + d[...].astype(F32)
    out_ref[...] = total.astype(BF)


def adam_kernel(total_rows):
    def kernel(got_ref, weight_ref, first_ref, second_ref, grad_ref, out_ref):
        total = got_ref[0].astype(F32)
        for k in range(1, got_ref.shape[0]):
            total = total + got_ref[k].astype(F32)
        grad = total / total_rows
        grad_ref[...] = grad
        first = first_ref[...] + (1.0 - BETA_ONE) * grad
        second = second_ref[...] + (1.0 - BETA_TWO) * grad * grad
        step = first / CORR_ONE / (jnp.sqrt(second / CORR_TWO) + EPSILON)
        new = (weight_ref[...] - RATE * step).astype(BF)
        for k in range(out_ref.shape[0]):
            out_ref[k] = new

    return kernel


def next_other_kernel(spot_ref, x_ref, g0, g1, g2, g3, out_ref, whole_ref, sems):
    copies = load_whole(spot_ref, (g0, g1, g2, g3), whole_ref, sems)
    for copy in copies:
        copy.start()
    for copy in copies:
        copy.wait()
    whole = whole_ref[...].reshape(x_ref.shape[1], out_ref.shape[1])
    out_ref[...] = jnp.dot(x_ref[...], whole, preferred_element_type=F32).astype(BF)


def next_mine_kernel(x_ref, whole_ref, out_ref):
    out_ref[...] = jnp.dot(x_ref[...], whole_ref[...], preferred_element_type=F32).astype(BF)


def pair(mine, other, core):
    return jnp.where(core == 0, jnp.stack([mine, other]), jnp.stack([other, mine]))


def on_device(tokens, route, cotangent, weight, first_q, first_scale, second_q, second_scale):
    n_z = lax.axis_size("z")
    core = lax.axis_index("core")
    high = lax.axis_index("yh")
    y = high * 2 + lax.axis_index("yl")
    x = lax.axis_index("x")
    spot = jnp.stack([core, jnp.where(core == 0, x, y), jnp.where(core == 0, y, x)]).astype(jnp.int32)
    rows_here = route.shape[1]
    depth = tokens.shape[1]
    feature = cotangent.shape[2]
    total_rows = rows_here * 2 * N_Y * n_z * N_X
    owned = weight.shape[1]
    half = owned // 2
    block_shape = (n_z, half, feature)
    natural = (2, n_z, N_X, 2, half)

    def mine_of(array):
        return lax.dynamic_index_in_dim(array, core, 0, keepdims=False)

    def other_of(array):
        return lax.dynamic_index_in_dim(array, 1 - core, 0, keepdims=False)

    def part_of(array):
        return lax.dynamic_slice_in_dim(mine_of(array), high * half, half, 0)

    def over_z(blocks):
        return lax.all_to_all(blocks, "z", 0, 0, tiled=True)

    weight_part = part_of(weight)
    along_z = over_z(jnp.broadcast_to(weight_part.astype(BF)[None], block_shape))
    tokens_far, route_far, cot_far = swap(tokens), swap(route), swap(cotangent)
    tokens_b, route_b, route_far = lax.optimization_barrier((tokens, route, route_far))
    gathered = gather_blocks(along_z)
    route_mine = mine_of(route_b)
    route_other = other_of(route_b)

    def rows_of(routes, from_tokens):
        return call(
            rows_kernel,
            [((rows_here, depth), BF, VMEM), ((N_Y, N_X, n_z, half, rows_here), BF, ANY)],
            spot,
            routes[None],
            from_tokens,
            scratch=[pltpu.VMEM(natural + (rows_here,), BF), pltpu.SemaphoreType.DMA((N_Y * N_X,))],
            mib=16,
            places=[SMEM, VMEM, VMEM],
        )

    x_mine, across_mine = rows_of(route_mine, tokens_b)
    x_other, across_other = rows_of(mine_of(route_far), tokens_far)
    first_part = BETA_ONE * dequant(part_of(first_q)[None], part_of(first_scale)[None])[0]
    second_part = BETA_TWO * dequant(part_of(second_q)[None], part_of(second_scale)[None])[0]
    *gathered, x_mine, x_other, cot_far, first_part, second_part = lax.optimization_barrier(
        (*gathered, x_mine, x_other, cot_far, first_part, second_part)
    )

    b0, b1, b2, b3, dmine, dother, whole = call(
        gate_kernel,
        [((N_X,) + block_shape, BF, ANY)] * 4
        + [((rows_here, feature), BF, ANY)] * 2
        + [(natural + (feature,), BF, ANY)],
        spot,
        in_hbm(x_mine),
        in_hbm(x_other),
        in_hbm(cotangent),
        in_hbm(cot_far),
        in_hbm(across_mine),
        in_hbm(across_other),
        *gathered,
        scratch=[
            pltpu.VMEM(natural + (feature,), BF),
            pltpu.VMEM((2 * rows_here, depth), BF),
            pltpu.VMEM((2 * rows_here, feature), BF),
            pltpu.VMEM((2, N_Y, N_X, n_z, half, rows_here), BF),
            pltpu.VMEM((2 * rows_here, feature), BF),
            pltpu.VMEM((N_Y, N_X) + block_shape, BF),
            pltpu.SemaphoreType.DMA((7,)),
            pltpu.SemaphoreType.DMA((N_Y * N_X,)),
            pltpu.SemaphoreType.DMA((2, N_Y)),
            pltpu.SemaphoreType.DMA((N_Y,)),
        ],
        mib=24,
        places=[SMEM] + [ANY] * 10,
    )
    whole = whole.reshape(depth, feature)
    got = [shift(block, k, False) for block, k in ((b1, 1), (b3, 3), (b2, 2))]
    p0, p1, p2, p3 = call(sum_outer_kernel, [(block_shape, BF, VMEM)] * 4, b0, *got)
    got = [shift(block, k, True) for block, k in ((p1, 1), (p3, 3), (p2, 2))]
    (part,) = call(sum_inner_kernel, [(block_shape, BF, VMEM)], p0, *got)
    got_z = over_z(part)
    grad, new_blocks = call(
        adam_kernel(total_rows),
        [((half, feature), F32, VMEM), (block_shape, BF, VMEM)],
        got_z,
        weight_part,
        first_part,
        second_part,
    )
    new_along_z = over_z(new_blocks)
    new_along_z, grad, whole, dother = lax.optimization_barrier((new_along_z, grad, whole, dother))
    new_gathered = gather_blocks(new_along_z)

    mine_half = pair(grad, swap(grad), core)
    far_half = pair(cross(grad, False), cross(grad, True), core)
    both = jnp.where(
        high == 0,
        jnp.concatenate([mine_half, far_half], axis=1),
        jnp.concatenate([far_half, mine_half], axis=1),
    )
    step_dir, new_weight = adam_update(weight, both, first_q, first_scale, second_q, second_scale)
    other_whole = swap(whole)
    other_rows = swap(dother)
    (token_grad,) = call(
        token_kernel,
        [(tokens.shape, BF, VMEM)],
        jnp.stack([route_mine, route_other]),
        dmine,
        other_rows,
        whole,
        other_whole,
        scratch=[pltpu.VMEM((2, 256, feature), BF)],
        mib=14,
    )
    *new_gathered, step_dir, new_weight, token_grad = lax.optimization_barrier(
        (*new_gathered, step_dir, new_weight, token_grad)
    )

    next_other, new_whole = call(
        next_other_kernel,
        [((rows_here, feature), BF, VMEM), (natural + (feature,), BF, VMEM)],
        spot,
        x_other,
        *new_gathered,
        scratch=[pltpu.SemaphoreType.DMA((N_Y * N_X,))],
        places=[SMEM, VMEM] + [ANY] * 4,
    )
    next_other = swap(next_other)
    (next_mine,) = call(
        next_mine_kernel,
        [((rows_here, feature), BF, VMEM)],
        x_mine,
        new_whole.reshape(depth, feature),
    )
    next_gate = pair(next_mine, next_other, core)
    return (token_grad, step_dir, new_weight, next_gate)


def solution(mesh):
    split = Mesh(mesh.devices.reshape(2, 2, 2, 8, 4), ("yh", "core", "yl", "z", "x"))
    rep = ("yh", "core")
    ep = ("yl", "z", "x")
    every = rep + ep
    in_specs = (
        P(every, None),
        P(None, every),
        P(None, every, None),
        P(None, ep, None),
        P(None, ep, None),
        P(None, ep, None),
        P(None, ep, None),
        P(None, ep, None),
    )
    out_specs = (
        P(every, None),
        P(None, ep, None),
        P(None, ep, None),
        P(None, every, None),
    )
    return jax.shard_map(
        on_device, mesh=split, in_specs=in_specs, out_specs=out_specs, check_vma=False
    )
```

```python
import jax
import jax.numpy as jnp
from jax import lax
from jax.experimental import pallas as pl
from jax.experimental.pallas import tpu as pltpu
from jax.sharding import Mesh
from jax.sharding import PartitionSpec as P

QBLOCK = 128

BETA_ONE = 0.9
BETA_TWO = 0.95
CORR_ONE = 1.0 - 0.9**10
CORR_TWO = 1.0 - 0.95**10
EPSILON = 1e-08
RATE = 0.002

BF = jnp.bfloat16
F32 = jnp.float32
AXES = ("yh", "core", "yl", "z", "x")
N_Y = 4
N_X = 4


def dequant(quant, scale):
    shaped = quant.astype(F32).reshape(quant.shape[0], quant.shape[1], -1, QBLOCK)
    return (shaped * scale[..., None]).reshape(quant.shape)


def adam_update(weight, grad, first_q, first_scale, second_q, second_scale):
    first = BETA_ONE * dequant(first_q, first_scale) + (1.0 - BETA_ONE) * grad
    second = BETA_TWO * dequant(second_q, second_scale) + (1.0 - BETA_TWO) * grad * grad
    step = first / CORR_ONE / (jnp.sqrt(second / CORR_TWO) + EPSILON)
    return (step, weight - RATE * step)


def swap(value):
    return lax.ppermute(value, "core", [(0, 1), (1, 0)])


def cross(value):
    return lax.ppermute(value, "yh", [(0, 1), (1, 0)])


def shift(value, k, inner):
    n_z = lax.axis_size("z")

    def number(y, core, z, x):
        return (((y // 2 * 2 + core) * 2 + y % 2) * n_z + z) * N_X + x

    pairs = []
    for core in range(2):
        for y in range(N_Y):
            for z in range(n_z):
                for x in range(N_X):
                    if (core == 0) == inner:
                        target = number(y, core, z, (x + k) % N_X)
                    else:
                        target = number((y + k) % N_Y, core, z, x)
                    pairs.append((number(y, core, z, x), target))
    return lax.ppermute(value, AXES, pairs)


def place(spot_ref, j, k, away):
    core = spot_ref[0]
    outer = (spot_ref[2] + (j if away else N_Y - j)) % N_Y
    inner = (spot_ref[1] + (k if away else N_X - k)) % N_X
    y = jnp.where(core == 0, outer, inner)
    x = jnp.where(core == 0, inner, outer)
    return y % 2, x, y // 2


def in_hbm(value):
    return pltpu.with_memory_space_constraint(value, pltpu.HBM)


ANY = "any"
SMEM = "smem"
VMEM = "vmem"


def call(kernel, outs, *args, scratch=(), mib=8, places=None):
    spec = {
        ANY: pl.BlockSpec(memory_space=pl.ANY),
        SMEM: pl.BlockSpec(memory_space=pltpu.SMEM),
        VMEM: pl.BlockSpec(memory_space=pltpu.VMEM),
    }
    return pl.pallas_call(
        kernel,
        out_shape=[
            pltpu.HBM(shape, dtype) if where == ANY else jax.ShapeDtypeStruct(shape, dtype)
            for shape, dtype, where in outs
        ],
        in_specs=[spec[where] for where in (places or [VMEM] * len(args))],
        out_specs=[spec[where] for _, _, where in outs],
        scratch_shapes=list(scratch),
        compiler_params=pltpu.CompilerParams(vmem_limit_bytes=mib << 20),
    )(*args)


def pack_kernel(*refs):
    *in_refs, out_ref = refs
    for k, in_ref in enumerate(in_refs):
        out_ref[k] = in_ref[...]


def gather_blocks(block, beside=None):
    parts = [block] + [shift(block, k, True) for k in (1, 3, 2)]
    parts = [parts[0], parts[1], parts[3], parts[2]]
    if beside is not None:
        parts, beside = lax.optimization_barrier((parts, beside))
    (packed,) = call(pack_kernel, [((N_X,) + block.shape, BF, VMEM)], *parts)
    far = [shift(packed, k, False) for k in (1, 3, 2)]
    return [packed, far[0], far[2], far[1]], beside


def load_whole(spot_ref, block_refs, whole_ref, sems):
    copies = []
    for j in range(N_Y):
        for k in range(N_X):
            low, x, high = place(spot_ref, j, k, False)
            copies.append(
                pltpu.make_async_copy(
                    block_refs[j].at[k], whole_ref.at[low, :, x, high], sems.at[j * N_X + k]
                )
            )
    return copies


def rows_kernel(spot_ref, route_ref, tokens_ref, x_ref, across_ref, from_ref, rows_ref, buf_ref, in_sems, sems):
    count, depth = x_ref.shape
    low_n, n_z, n_x, high_n, rows, _ = buf_ref.shape
    step = 256
    core = spot_ref[0]
    load = pltpu.make_async_copy(tokens_ref, from_ref, in_sems.at[0])
    load.start()
    places = lax.broadcasted_iota(jnp.int32, (tokens_ref.shape[0], count), 0)
    hot = jnp.where(places == route_ref[...], 1.0, 0.0).astype(BF).T
    copies = []
    load.wait()
    for low in range(low_n):
        for d in range(low * depth // low_n, (low + 1) * depth // low_n, step):
            picked = jnp.dot(hot, from_ref[:, d : d + step], preferred_element_type=F32).astype(BF)
            rows_ref[:, d : d + step] = picked
            turned = picked.T
            for g in range(step // rows):
                index = d // rows + g
                high = index % high_n
                x = index // high_n % n_x
                z = index // high_n // n_x % n_z
                buf_ref[low, z, x, high] = turned[g * rows : (g + 1) * rows]
        for high in range(high_n):
            for x in range(n_x):
                y = 2 * high + low
                j = (jnp.where(core == 0, y, x) - spot_ref[2] + N_Y) % N_Y
                k = (jnp.where(core == 0, x, y) - spot_ref[1] + N_X) % N_X
                copies.append(
                    pltpu.make_async_copy(buf_ref.at[low, :, x, high], across_ref.at[j, k], sems.at[len(copies)])
                )
                copies[-1].start()
    copies.append(pltpu.make_async_copy(rows_ref, x_ref, in_sems.at[1]))
    copies[-1].start()
    for copy in copies:
        copy.wait()


def gate_kernel(spot_ref, mine_ref, other_ref, cot_mine_ref, cot_other_ref,
                across_mine_ref, across_other_ref, g0, g1, g2, g3, o0, o1, o2, o3, dmine_ref, dother_ref, whole_out_ref,
                whole_ref, x_ref, cot_ref, turned_ref, d_ref, part_ref, in_sems, w_sems, t_sems, out_sems):
    low_n, n_z, n_x, high_n, rows, feature = whole_ref.shape
    count, depth = mine_ref.shape
    step = 256
    core = spot_ref[0]
    w_copies = load_whole(spot_ref, (g0, g1, g2, g3), whole_ref, w_sems)
    loads = [
        pltpu.make_async_copy(mine_ref, x_ref.at[pl.ds(0, count)], in_sems.at[0]),
        pltpu.make_async_copy(cot_mine_ref.at[core], cot_ref.at[pl.ds(0, count)], in_sems.at[1]),
        pltpu.make_async_copy(other_ref, x_ref.at[pl.ds(count, count)], in_sems.at[2]),
        pltpu.make_async_copy(cot_other_ref.at[core], cot_ref.at[pl.ds(count, count)], in_sems.at[3]),
    ]
    order = (1, 3, 2, 0)
    t_loads = [
        [
            pltpu.make_async_copy(ref.at[j], turned_ref.at[half, j], t_sems.at[half, j])
            for half, ref in enumerate((across_mine_ref, across_other_ref))
        ]
        for j in order
    ]
    for copy in w_copies + loads[:2]:
        copy.start()
    for copy in w_copies:
        copy.wait()
    for copy in loads[2:] + [copy for pair in t_loads for copy in pair]:
        copy.start()
    whole_out = pltpu.make_async_copy(whole_ref, whole_out_ref, in_sems.at[4])
    whole_out.start()
    whole = whole_ref[...].reshape(depth, feature)
    outs = [whole_out]
    for half in range(2):
        loads[2 * half].wait()
        loads[2 * half + 1].wait()
        for r in range(half * count, (half + 1) * count, step):
            gate = jnp.dot(x_ref[r : r + step, :], whole, preferred_element_type=F32)
            sig = jax.nn.sigmoid(gate)
            cot = cot_ref[r : r + step, :].astype(F32)
            d_ref[r : r + step, :] = (cot * sig * (1.0 + gate * (1.0 - sig))).astype(BF)
        outs.append(
            pltpu.make_async_copy(
                d_ref.at[pl.ds(half * count, count)], (dmine_ref, dother_ref)[half], in_sems.at[5 + half]
            )
        )
        outs[-1].start()
    for i, j in enumerate(order):
        for copy in t_loads[i]:
            copy.wait()
        for k in range(0, N_X, 2):
            part = None
            for half in range(2):
                turned = turned_ref[half, j, k : k + 2].reshape(2 * n_z * rows, count)
                product = jnp.dot(turned, d_ref[half * count : (half + 1) * count, :], preferred_element_type=F32)
                part = product if part is None else part + product
            part = part.astype(BF).reshape(2, n_z, rows, feature)
            if j:
                part_ref[j - 1, k : k + 2] = part
            else:
                o0[k : k + 2] = part
        if j:
            outs.append(pltpu.make_async_copy(part_ref.at[j - 1], (o1, o2, o3)[j - 1], out_sems.at[j - 1]))
            outs[-1].start()
    for copy in outs:
        copy.wait()


def token_kernel(routes_ref, dmine_ref, dother_ref, whole_ref, other_ref, out_ref, placed_ref):
    count = dmine_ref.shape[0]
    step = 256
    turned = (((1,), (1,)), ((), ()))
    for t in range(0, out_ref.shape[0], step):
        places = t + lax.broadcasted_iota(jnp.int32, (step, count), 0)
        for e, d_ref in enumerate((dmine_ref, dother_ref)):
            hot = jnp.where(places == routes_ref[e : e + 1, :], 1.0, 0.0).astype(BF)
            placed_ref[e] = jnp.dot(hot, d_ref[...], preferred_element_type=F32).astype(BF)
        for d in range(0, out_ref.shape[1], 2 * step):
            at = slice(d, d + 2 * step)
            total = lax.dot_general(placed_ref[0], whole_ref[at, :], turned, preferred_element_type=F32)
            total = total + lax.dot_general(placed_ref[1], other_ref[at, :], turned, preferred_element_type=F32)
            out_ref[t : t + step, at] = total.astype(BF)


def sum_outer_kernel(a, b, c, d, o0, o1, o2, o3):
    for k, out_ref in enumerate((o0, o1, o2, o3)):
        total = a[k].astype(F32) + b[k].astype(F32) + c[k].astype(F32) + d[k].astype(F32)
        out_ref[...] = total.astype(BF)


def sum_inner_kernel(a, b, c, d, out_ref):
    total = a[...].astype(F32) + b[...].astype(F32) + c[...].astype(F32) + d[...].astype(F32)
    out_ref[...] = total.astype(BF)


def adam_kernel(total_rows):
    def kernel(got_ref, weight_ref, first_ref, second_ref, grad_ref, out_ref):
        total = got_ref[0].astype(F32)
        for k in range(1, got_ref.shape[0]):
            total = total + got_ref[k].astype(F32)
        grad = total / total_rows
        grad_ref[...] = grad
        first = first_ref[...] + (1.0 - BETA_ONE) * grad
        second = second_ref[...] + (1.0 - BETA_TWO) * grad * grad
        step = first / CORR_ONE / (jnp.sqrt(second / CORR_TWO) + EPSILON)
        new = (weight_ref[...] - RATE * step).astype(BF)
        for k in range(out_ref.shape[0]):
            out_ref[k] = new

    return kernel


def next_other_kernel(spot_ref, x_ref, g0, g1, g2, g3, out_ref, whole_ref, sems):
    copies = load_whole(spot_ref, (g0, g1, g2, g3), whole_ref, sems)
    for copy in copies:
        copy.start()
    for copy in copies:
        copy.wait()
    whole = whole_ref[...].reshape(x_ref.shape[1], out_ref.shape[1])
    out_ref[...] = jnp.dot(x_ref[...], whole, preferred_element_type=F32).astype(BF)


def next_mine_kernel(x_ref, whole_ref, out_ref):
    out_ref[...] = jnp.dot(x_ref[...], whole_ref[...], preferred_element_type=F32).astype(BF)


def pair(mine, other, core):
    return jnp.where(core == 0, jnp.stack([mine, other]), jnp.stack([other, mine]))


def on_device(tokens, route, cotangent, weight, first_q, first_scale, second_q, second_scale):
    n_z = lax.axis_size("z")
    core = lax.axis_index("core")
    high = lax.axis_index("yh")
    y = high * 2 + lax.axis_index("yl")
    x = lax.axis_index("x")
    spot = jnp.stack([core, jnp.where(core == 0, x, y), jnp.where(core == 0, y, x)]).astype(jnp.int32)
    rows_here = route.shape[1]
    depth = tokens.shape[1]
    feature = cotangent.shape[2]
    total_rows = rows_here * 2 * N_Y * n_z * N_X
    owned = weight.shape[1]
    half = owned // 2
    block_shape = (n_z, half, feature)
    natural = (2, n_z, N_X, 2, half)

    def mine_of(array):
        return lax.dynamic_index_in_dim(array, core, 0, keepdims=False)

    def other_of(array):
        return lax.dynamic_index_in_dim(array, 1 - core, 0, keepdims=False)

    def part_of(array):
        return lax.dynamic_slice_in_dim(mine_of(array), high * half, half, 0)

    def over_z(blocks):
        return lax.all_to_all(blocks, "z", 0, 0, tiled=True)

    weight_part = part_of(weight)
    along_z = over_z(jnp.broadcast_to(weight_part.astype(BF)[None], block_shape))
    tokens_far, route_far, cot_far = swap(tokens), swap(route), swap(cotangent)
    gathered, _ = gather_blocks(along_z)
    route_mine = mine_of(route)
    route_other = other_of(route)

    def rows_of(routes, from_tokens):
        return call(
            rows_kernel,
            [((rows_here, depth), BF, ANY), ((N_Y, N_X, n_z, half, rows_here), BF, ANY)],
            spot,
            routes[None],
            in_hbm(from_tokens),
            scratch=[
                pltpu.VMEM(tokens.shape, BF),
                pltpu.VMEM((rows_here, depth), BF),
                pltpu.VMEM(natural + (rows_here,), BF),
                pltpu.SemaphoreType.DMA((2,)),
                pltpu.SemaphoreType.DMA((N_Y * N_X,)),
            ],
            mib=16,
            places=[SMEM, VMEM, ANY],
        )

    x_mine, across_mine = rows_of(route_mine, tokens)
    x_other, across_other = rows_of(mine_of(route_far), tokens_far)
    first_part = BETA_ONE * dequant(part_of(first_q)[None], part_of(first_scale)[None])[0]
    second_part = BETA_TWO * dequant(part_of(second_q)[None], part_of(second_scale)[None])[0]
    *gathered, x_mine, x_other, cot_far, first_part, second_part = lax.optimization_barrier(
        (*gathered, x_mine, x_other, cot_far, first_part, second_part)
    )

    b0, b1, b2, b3, dmine, dother, whole = call(
        gate_kernel,
        [((N_X,) + block_shape, BF, VMEM)]
        + [((N_X,) + block_shape, BF, ANY)] * 3
        + [((rows_here, feature), BF, ANY)] * 2
        + [(natural + (feature,), BF, ANY)],
        spot,
        in_hbm(x_mine),
        in_hbm(x_other),
        in_hbm(cotangent),
        cot_far,
        in_hbm(across_mine),
        in_hbm(across_other),
        *gathered,
        scratch=[
            pltpu.VMEM(natural + (feature,), BF),
            pltpu.VMEM((2 * rows_here, depth), BF),
            pltpu.VMEM((2 * rows_here, feature), BF),
            pltpu.VMEM((2, N_Y, N_X, n_z, half, rows_here), BF),
            pltpu.VMEM((2 * rows_here, feature), BF),
            pltpu.VMEM((N_Y - 1, N_X) + block_shape, BF),
            pltpu.SemaphoreType.DMA((7,)),
            pltpu.SemaphoreType.DMA((N_Y * N_X,)),
            pltpu.SemaphoreType.DMA((2, N_Y)),
            pltpu.SemaphoreType.DMA((N_Y - 1,)),
        ],
        mib=24,
        places=[SMEM] + [ANY] * 10,
    )
    whole = whole.reshape(depth, feature)
    got = [shift(block, k, False) for block, k in ((b1, 1), (b3, 3), (b2, 2))]
    other_whole = swap(whole)
    other_rows = swap(dother)
    (token_grad,) = call(
        token_kernel,
        [(tokens.shape, BF, VMEM)],
        jnp.stack([route_mine, route_other]),
        dmine,
        other_rows,
        whole,
        other_whole,
        scratch=[pltpu.VMEM((2, 256, feature), BF)],
        mib=14,
    )
    *got, token_grad = lax.optimization_barrier((*got, token_grad))
    p0, p1, p2, p3 = call(sum_outer_kernel, [(block_shape, BF, VMEM)] * 4, b0, *got)
    got = [shift(block, k, True) for block, k in ((p1, 1), (p3, 3), (p2, 2))]
    (part,) = call(sum_inner_kernel, [(block_shape, BF, VMEM)], p0, *got)
    got_z = over_z(part)
    grad, new_blocks = call(
        adam_kernel(total_rows),
        [((half, feature), F32, VMEM), (block_shape, BF, VMEM)],
        got_z,
        weight_part,
        first_part,
        second_part,
    )
    new_along_z = over_z(new_blocks)

    new_along_z, grad = lax.optimization_barrier((new_along_z, grad))
    new_gathered, far_grad = gather_blocks(new_along_z, cross(grad))
    owned_grad = jnp.where(
        high == 0, jnp.concatenate([grad, far_grad], axis=0), jnp.concatenate([far_grad, grad], axis=0)
    )
    both = pair(owned_grad, swap(owned_grad), core)
    step_dir, new_weight = adam_update(weight, both, first_q, first_scale, second_q, second_scale)
    *new_gathered, step_dir, new_weight = lax.optimization_barrier((*new_gathered, step_dir, new_weight))

    next_other, new_whole = call(
        next_other_kernel,
        [((rows_here, feature), BF, VMEM), (natural + (feature,), BF, VMEM)],
        spot,
        x_other,
        *new_gathered,
        scratch=[pltpu.SemaphoreType.DMA((N_Y * N_X,))],
        places=[SMEM, VMEM] + [ANY] * 4,
    )
    next_other = swap(next_other)
    (next_mine,) = call(
        next_mine_kernel,
        [((rows_here, feature), BF, VMEM)],
        x_mine,
        new_whole.reshape(depth, feature),
    )
    next_gate = pair(next_mine, next_other, core)
    return (token_grad, step_dir, new_weight, next_gate)


def solution(mesh):
    split = Mesh(mesh.devices.reshape(2, 2, 2, 8, 4), ("yh", "core", "yl", "z", "x"))
    rep = ("yh", "core")
    ep = ("yl", "z", "x")
    every = rep + ep
    in_specs = (
        P(every, None),
        P(None, every),
        P(None, every, None),
        P(None, ep, None),
        P(None, ep, None),
        P(None, ep, None),
        P(None, ep, None),
        P(None, ep, None),
    )
    out_specs = (
        P(every, None),
        P(None, ep, None),
        P(None, ep, None),
        P(None, every, None),
    )
    return jax.shard_map(
        on_device, mesh=split, in_specs=in_specs, out_specs=out_specs, check_vma=False
    )
```

```python
import jax
import jax.numpy as jnp
from jax import lax
from jax.experimental import pallas as pl
from jax.experimental.pallas import tpu as pltpu
from jax.sharding import Mesh
from jax.sharding import PartitionSpec as P

QBLOCK = 128

BETA_ONE = 0.9
BETA_TWO = 0.95
CORR_ONE = 1.0 - 0.9**10
CORR_TWO = 1.0 - 0.95**10
EPSILON = 1e-08
RATE = 0.002

BF = jnp.bfloat16
F32 = jnp.float32
AXES = ("yh", "core", "yl", "z", "x")
N_Y = 4
N_X = 4


def dequant(quant, scale):
    shaped = quant.astype(F32).reshape(quant.shape[0], quant.shape[1], -1, QBLOCK)
    return (shaped * scale[..., None]).reshape(quant.shape)


def adam_update(weight, grad, first_q, first_scale, second_q, second_scale):
    first = BETA_ONE * dequant(first_q, first_scale) + (1.0 - BETA_ONE) * grad
    second = BETA_TWO * dequant(second_q, second_scale) + (1.0 - BETA_TWO) * grad * grad
    step = first / CORR_ONE / (jnp.sqrt(second / CORR_TWO) + EPSILON)
    return (step, weight - RATE * step)


def swap(value):
    return lax.ppermute(value, "core", [(0, 1), (1, 0)])


def cross(value):
    return lax.ppermute(value, "yh", [(0, 1), (1, 0)])


def shift(value, k, inner):
    n_z = lax.axis_size("z")

    def number(y, core, z, x):
        return (((y // 2 * 2 + core) * 2 + y % 2) * n_z + z) * N_X + x

    pairs = []
    for core in range(2):
        for y in range(N_Y):
            for z in range(n_z):
                for x in range(N_X):
                    if (core == 0) == inner:
                        target = number(y, core, z, (x + k) % N_X)
                    else:
                        target = number((y + k) % N_Y, core, z, x)
                    pairs.append((number(y, core, z, x), target))
    return lax.ppermute(value, AXES, pairs)


def place(spot_ref, j, k, away):
    core = spot_ref[0]
    outer = (spot_ref[2] + (j if away else N_Y - j)) % N_Y
    inner = (spot_ref[1] + (k if away else N_X - k)) % N_X
    y = jnp.where(core == 0, outer, inner)
    x = jnp.where(core == 0, inner, outer)
    return y % 2, x, y // 2


def in_hbm(value):
    return pltpu.with_memory_space_constraint(value, pltpu.HBM)


ANY = "any"
SMEM = "smem"
VMEM = "vmem"


def call(kernel, outs, *args, scratch=(), mib=8, places=None):
    spec = {
        ANY: pl.BlockSpec(memory_space=pl.ANY),
        SMEM: pl.BlockSpec(memory_space=pltpu.SMEM),
        VMEM: pl.BlockSpec(memory_space=pltpu.VMEM),
    }
    return pl.pallas_call(
        kernel,
        out_shape=[
            pltpu.HBM(shape, dtype) if where == ANY else jax.ShapeDtypeStruct(shape, dtype)
            for shape, dtype, where in outs
        ],
        in_specs=[spec[where] for where in (places or [VMEM] * len(args))],
        out_specs=[spec[where] for _, _, where in outs],
        scratch_shapes=list(scratch),
        compiler_params=pltpu.CompilerParams(vmem_limit_bytes=mib << 20),
    )(*args)


def pack_kernel(*refs):
    *in_refs, out_ref = refs
    for k, in_ref in enumerate(in_refs):
        out_ref[k] = in_ref[...]


def gather_blocks(block, beside=None):
    parts = [block] + [shift(block, k, True) for k in (1, 3, 2)]
    parts = [parts[0], parts[1], parts[3], parts[2]]
    if beside is not None:
        parts, beside = lax.optimization_barrier((parts, beside))
    (packed,) = call(pack_kernel, [((N_X,) + block.shape, BF, VMEM)], *parts)
    far = [shift(packed, k, False) for k in (1, 3, 2)]
    return [packed, far[0], far[2], far[1]], beside


def load_whole(spot_ref, block_refs, whole_ref, sems):
    copies = []
    for j in range(N_Y):
        for k in range(N_X):
            low, x, high = place(spot_ref, j, k, False)
            copies.append(
                pltpu.make_async_copy(
                    block_refs[j].at[k], whole_ref.at[low, :, x, high], sems.at[j * N_X + k]
                )
            )
    return copies


def rows_kernel(spot_ref, route_ref, tokens_ref, x_ref, across_ref, from_ref, rows_ref, buf_ref, in_sems, sems):
    count, depth = x_ref.shape
    low_n, n_z, n_x, high_n, rows, _ = buf_ref.shape
    step = 256
    core = spot_ref[0]
    load = pltpu.make_async_copy(tokens_ref, from_ref, in_sems.at[0])
    load.start()
    places = lax.broadcasted_iota(jnp.int32, (tokens_ref.shape[0], count), 0)
    hot = jnp.where(places == route_ref[...], 1.0, 0.0).astype(BF).T
    copies = []
    load.wait()
    for low in range(low_n):
        for d in range(low * depth // low_n, (low + 1) * depth // low_n, step):
            picked = jnp.dot(hot, from_ref[:, d : d + step], preferred_element_type=F32).astype(BF)
            rows_ref[:, d : d + step] = picked
            turned = picked.T
            for g in range(step // rows):
                index = d // rows + g
                high = index % high_n
                x = index // high_n % n_x
                z = index // high_n // n_x % n_z
                buf_ref[low, z, x, high] = turned[g * rows : (g + 1) * rows]
        for high in range(high_n):
            for x in range(n_x):
                y = 2 * high + low
                j = (jnp.where(core == 0, y, x) - spot_ref[2] + N_Y) % N_Y
                k = (jnp.where(core == 0, x, y) - spot_ref[1] + N_X) % N_X
                copies.append(
                    pltpu.make_async_copy(buf_ref.at[low, :, x, high], across_ref.at[j, k], sems.at[len(copies)])
                )
                copies[-1].start()
    copies.append(pltpu.make_async_copy(rows_ref, x_ref, in_sems.at[1]))
    copies[-1].start()
    for copy in copies:
        copy.wait()


def gate_kernel(spot_ref, mine_ref, other_ref, cot_mine_ref, cot_other_ref,
                across_mine_ref, across_other_ref, g0, g1, g2, g3, o0, o1, o2, o3, dmine_ref, dother_ref, whole_out_ref,
                whole_ref, x_ref, cot_ref, turned_ref, d_ref, part_ref, in_sems, w_sems, t_sems, out_sems):
    low_n, n_z, n_x, high_n, rows, feature = whole_ref.shape
    count, depth = mine_ref.shape
    step = 256
    core = spot_ref[0]
    w_copies = load_whole(spot_ref, (g0, g1, g2, g3), whole_ref, w_sems)
    loads = [
        pltpu.make_async_copy(mine_ref, x_ref.at[pl.ds(0, count)], in_sems.at[0]),
        pltpu.make_async_copy(cot_mine_ref.at[core], cot_ref.at[pl.ds(0, count)], in_sems.at[1]),
        pltpu.make_async_copy(other_ref, x_ref.at[pl.ds(count, count)], in_sems.at[2]),
        pltpu.make_async_copy(cot_other_ref.at[core], cot_ref.at[pl.ds(count, count)], in_sems.at[3]),
    ]
    order = (1, 3, 2, 0)
    t_loads = [
        [
            pltpu.make_async_copy(ref.at[j], turned_ref.at[half, j], t_sems.at[half, j])
            for half, ref in enumerate((across_mine_ref, across_other_ref))
        ]
        for j in order
    ]
    for copy in w_copies + loads[:2]:
        copy.start()
    for copy in w_copies:
        copy.wait()
    for copy in loads[2:] + [copy for pair in t_loads for copy in pair]:
        copy.start()
    whole_out = pltpu.make_async_copy(whole_ref, whole_out_ref, in_sems.at[4])
    whole_out.start()
    whole = whole_ref[...].reshape(depth, feature)
    outs = [whole_out]
    for half in range(2):
        loads[2 * half].wait()
        loads[2 * half + 1].wait()
        for r in range(half * count, (half + 1) * count, step):
            gate = jnp.dot(x_ref[r : r + step, :], whole, preferred_element_type=F32)
            sig = jax.nn.sigmoid(gate)
            cot = cot_ref[r : r + step, :].astype(F32)
            d_ref[r : r + step, :] = (cot * sig * (1.0 + gate * (1.0 - sig))).astype(BF)
        outs.append(
            pltpu.make_async_copy(
                d_ref.at[pl.ds(half * count, count)], (dmine_ref, dother_ref)[half], in_sems.at[5 + half]
            )
        )
        outs[-1].start()
    for i, j in enumerate(order):
        for copy in t_loads[i]:
            copy.wait()
        for k in range(0, N_X, 2):
            part = None
            for half in range(2):
                turned = turned_ref[half, j, k : k + 2].reshape(2 * n_z * rows, count)
                product = jnp.dot(turned, d_ref[half * count : (half + 1) * count, :], preferred_element_type=F32)
                part = product if part is None else part + product
            part = part.astype(BF).reshape(2, n_z, rows, feature)
            if j:
                part_ref[j - 1, k : k + 2] = part
            else:
                o0[k : k + 2] = part
        if j:
            outs.append(pltpu.make_async_copy(part_ref.at[j - 1], (o1, o2, o3)[j - 1], out_sems.at[j - 1]))
            outs[-1].start()
    for copy in outs:
        copy.wait()


def token_kernel(routes_ref, dmine_ref, dother_ref, whole_ref, other_ref, out_ref, placed_ref):
    count = dmine_ref.shape[0]
    step = 256
    turned = (((1,), (1,)), ((), ()))
    for t in range(0, out_ref.shape[0], step):
        places = t + lax.broadcasted_iota(jnp.int32, (step, count), 0)
        for e, d_ref in enumerate((dmine_ref, dother_ref)):
            hot = jnp.where(places == routes_ref[e : e + 1, :], 1.0, 0.0).astype(BF)
            placed_ref[e] = jnp.dot(hot, d_ref[...], preferred_element_type=F32).astype(BF)
        for d in range(0, out_ref.shape[1], 2 * step):
            at = slice(d, d + 2 * step)
            total = lax.dot_general(placed_ref[0], whole_ref[at, :], turned, preferred_element_type=F32)
            total = total + lax.dot_general(placed_ref[1], other_ref[at, :], turned, preferred_element_type=F32)
            out_ref[t : t + step, at] = total.astype(BF)


def sum_outer_kernel(a, b, c, d, o0, o1, o2, o3):
    for k, out_ref in enumerate((o0, o1, o2, o3)):
        total = a[k].astype(F32) + b[k].astype(F32) + c[k].astype(F32) + d[k].astype(F32)
        out_ref[...] = total.astype(BF)


def sum_inner_kernel(a, b, c, d, out_ref):
    total = a[...].astype(F32) + b[...].astype(F32) + c[...].astype(F32) + d[...].astype(F32)
    out_ref[...] = total.astype(BF)


def adam_kernel(total_rows):
    def kernel(got_ref, weight_ref, first_ref, second_ref, grad_ref, out_ref):
        total = got_ref[0].astype(F32)
        for k in range(1, got_ref.shape[0]):
            total = total + got_ref[k].astype(F32)
        grad = total / total_rows
        grad_ref[...] = grad
        first = first_ref[...] + (1.0 - BETA_ONE) * grad
        second = second_ref[...] + (1.0 - BETA_TWO) * grad * grad
        step = first / CORR_ONE / (jnp.sqrt(second / CORR_TWO) + EPSILON)
        new = (weight_ref[...] - RATE * step).astype(BF)
        for k in range(out_ref.shape[0]):
            out_ref[k] = new

    return kernel


def next_other_kernel(spot_ref, x_ref, g0, g1, g2, g3, out_ref, whole_ref, sems):
    copies = load_whole(spot_ref, (g0, g1, g2, g3), whole_ref, sems)
    for copy in copies:
        copy.start()
    for copy in copies:
        copy.wait()
    whole = whole_ref[...].reshape(x_ref.shape[1], out_ref.shape[1])
    out_ref[...] = jnp.dot(x_ref[...], whole, preferred_element_type=F32).astype(BF)


def next_mine_kernel(x_ref, whole_ref, out_ref):
    out_ref[...] = jnp.dot(x_ref[...], whole_ref[...], preferred_element_type=F32).astype(BF)


def pair(mine, other, core):
    return jnp.where(core == 0, jnp.stack([mine, other]), jnp.stack([other, mine]))


def on_device(tokens, route, cotangent, weight, first_q, first_scale, second_q, second_scale):
    n_z = lax.axis_size("z")
    core = lax.axis_index("core")
    high = lax.axis_index("yh")
    y = high * 2 + lax.axis_index("yl")
    x = lax.axis_index("x")
    spot = jnp.stack([core, jnp.where(core == 0, x, y), jnp.where(core == 0, y, x)]).astype(jnp.int32)
    rows_here = route.shape[1]
    depth = tokens.shape[1]
    feature = cotangent.shape[2]
    total_rows = rows_here * 2 * N_Y * n_z * N_X
    owned = weight.shape[1]
    half = owned // 2
    block_shape = (n_z, half, feature)
    natural = (2, n_z, N_X, 2, half)

    def mine_of(array):
        return lax.dynamic_index_in_dim(array, core, 0, keepdims=False)

    def other_of(array):
        return lax.dynamic_index_in_dim(array, 1 - core, 0, keepdims=False)

    def part_of(array):
        return lax.dynamic_slice_in_dim(mine_of(array), high * half, half, 0)

    def over_z(blocks):
        return lax.all_to_all(blocks, "z", 0, 0, tiled=True)

    weight_part = part_of(weight)
    along_z = over_z(jnp.broadcast_to(weight_part.astype(BF)[None], block_shape))
    tokens_far, route_far, cot_far = swap(tokens), swap(route), swap(cotangent)
    gathered, _ = gather_blocks(along_z)
    route_mine = mine_of(route)
    route_other = other_of(route)

    def rows_of(routes, from_tokens):
        return call(
            rows_kernel,
            [((rows_here, depth), BF, ANY), ((N_Y, N_X, n_z, half, rows_here), BF, ANY)],
            spot,
            routes[None],
            in_hbm(from_tokens),
            scratch=[
                pltpu.VMEM(tokens.shape, BF),
                pltpu.VMEM((rows_here, depth), BF),
                pltpu.VMEM(natural + (rows_here,), BF),
                pltpu.SemaphoreType.DMA((2,)),
                pltpu.SemaphoreType.DMA((N_Y * N_X,)),
            ],
            mib=16,
            places=[SMEM, VMEM, ANY],
        )

    x_mine, across_mine = rows_of(route_mine, tokens)
    x_other, across_other = rows_of(mine_of(route_far), tokens_far)
    first_part = BETA_ONE * dequant(part_of(first_q)[None], part_of(first_scale)[None])[0]
    second_part = BETA_TWO * dequant(part_of(second_q)[None], part_of(second_scale)[None])[0]
    *gathered, x_mine, x_other, cot_far, first_part, second_part = lax.optimization_barrier(
        (*gathered, x_mine, x_other, cot_far, first_part, second_part)
    )

    b0, b1, b2, b3, dmine, dother, whole = call(
        gate_kernel,
        [((N_X,) + block_shape, BF, VMEM)]
        + [((N_X,) + block_shape, BF, ANY)] * 3
        + [((rows_here, feature), BF, ANY)] * 2
        + [(natural + (feature,), BF, ANY)],
        spot,
        in_hbm(x_mine),
        in_hbm(x_other),
        in_hbm(cotangent),
        cot_far,
        in_hbm(across_mine),
        in_hbm(across_other),
        *gathered,
        scratch=[
            pltpu.VMEM(natural + (feature,), BF),
            pltpu.VMEM((2 * rows_here, depth), BF),
            pltpu.VMEM((2 * rows_here, feature), BF),
            pltpu.VMEM((2, N_Y, N_X, n_z, half, rows_here), BF),
            pltpu.VMEM((2 * rows_here, feature), BF),
            pltpu.VMEM((N_Y - 1, N_X) + block_shape, BF),
            pltpu.SemaphoreType.DMA((7,)),
            pltpu.SemaphoreType.DMA((N_Y * N_X,)),
            pltpu.SemaphoreType.DMA((2, N_Y)),
            pltpu.SemaphoreType.DMA((N_Y - 1,)),
        ],
        mib=24,
        places=[SMEM] + [ANY] * 10,
    )
    whole = whole.reshape(depth, feature)
    got = [shift(block, k, False) for block, k in ((b1, 1), (b3, 3), (b2, 2))]
    other_whole = swap(whole)
    other_rows = swap(dother)
    (token_grad,) = call(
        token_kernel,
        [(tokens.shape, BF, VMEM)],
        jnp.stack([route_mine, route_other]),
        dmine,
        other_rows,
        whole,
        other_whole,
        scratch=[pltpu.VMEM((2, 256, feature), BF)],
        mib=14,
    )
    *got, token_grad, owned_part = lax.optimization_barrier((*got, token_grad, part_of(weight)))
    p0, p1, p2, p3 = call(sum_outer_kernel, [(block_shape, BF, VMEM)] * 4, b0, *got)
    got = [shift(block, k, True) for block, k in ((p1, 1), (p3, 3), (p2, 2))]
    (part,) = call(sum_inner_kernel, [(block_shape, BF, VMEM)], p0, *got)
    got_z = over_z(part)
    grad, new_blocks = call(
        adam_kernel(total_rows),
        [((half, feature), F32, VMEM), (block_shape, BF, VMEM)],
        got_z,
        owned_part,
        first_part,
        second_part,
    )
    new_along_z = over_z(new_blocks)

    new_along_z, grad = lax.optimization_barrier((new_along_z, grad))
    new_gathered, far_grad = gather_blocks(new_along_z, cross(grad))
    owned_grad = jnp.where(
        high == 0, jnp.concatenate([grad, far_grad], axis=0), jnp.concatenate([far_grad, grad], axis=0)
    )
    both = pair(owned_grad, swap(owned_grad), core)
    step_dir, new_weight = adam_update(weight, both, first_q, first_scale, second_q, second_scale)
    *new_gathered, step_dir, new_weight = lax.optimization_barrier((*new_gathered, step_dir, new_weight))

    next_other, new_whole = call(
        next_other_kernel,
        [((rows_here, feature), BF, VMEM), (natural + (feature,), BF, VMEM)],
        spot,
        x_other,
        *new_gathered,
        scratch=[pltpu.SemaphoreType.DMA((N_Y * N_X,))],
        places=[SMEM, VMEM] + [ANY] * 4,
    )
    next_other = swap(next_other)
    (next_mine,) = call(
        next_mine_kernel,
        [((rows_here, feature), BF, VMEM)],
        x_mine,
        new_whole.reshape(depth, feature),
    )
    next_gate = pair(next_mine, next_other, core)
    return (token_grad, step_dir, new_weight, next_gate)


def solution(mesh):
    split = Mesh(mesh.devices.reshape(2, 2, 2, 8, 4), ("yh", "core", "yl", "z", "x"))
    rep = ("yh", "core")
    ep = ("yl", "z", "x")
    every = rep + ep
    in_specs = (
        P(every, None),
        P(None, every),
        P(None, every, None),
        P(None, ep, None),
        P(None, ep, None),
        P(None, ep, None),
        P(None, ep, None),
        P(None, ep, None),
    )
    out_specs = (
        P(every, None),
        P(None, ep, None),
        P(None, ep, None),
        P(None, every, None),
    )
    return jax.shard_map(
        on_device, mesh=split, in_specs=in_specs, out_specs=out_specs, check_vma=False
    )
```
